32 devices in a mesh: groups: 2 (over x), seq: 16 (over z, y, core).
Axes of the slice: x: 2, y: 2, z: 4, core: 2. Of those that a mesh axis runs over, the one named last changes fastest.
Arguments:
- features: bfloat16 [16384, 768], P(('groups', 'seq')), parts along dimension 0, may hold values from -54 to 54
- bases: int32 [16384], P(('groups', 'seq')), parts along dimension 0, may hold values from 0 to 3
- base_table: bfloat16 [4, 768], replicated, may hold values from -3 to 3
- norm_gain: bfloat16 [768], replicated, may hold values from 0.25 to 1.75
- conv_weight: bfloat16 [5, 768, 768], replicated, may hold values from -0.09375 to 0.09375
- donor_proj: bfloat16 [768, 768], replicated, may hold values from -0.21875 to 0.21875
- acceptor_proj: bfloat16 [768, 768], replicated, may hold values from -0.21875 to 0.21875
- track_weight: bfloat16 [256, 768], replicated, may hold values from -0.375 to 0.375
- donor_offset: int32 [8192], P(('groups', 'seq')), parts along dimension 0, may hold values from 0 to 511
- acceptor_shard: int32 [8192, 1], P(('groups', 'seq')), parts along dimension 0, may hold values from 0 to 15; in each aligned block of 256 rows (0 to 255, 256 to 511, ...) at most 32 rows name the same one
- acceptor_offset: int32 [8192], P(('groups', 'seq')), parts along dimension 0, may hold values from 0 to 511
- junction_cotangent: bfloat16 [8192, 256], P(('groups', 'seq')), parts along dimension 0, may hold values from -6 to 6
Outputs:
- block_out: bfloat16 [16384, 768], P(('groups', 'seq')), parts along dimension 0
- head_grad: float32 [16384, 768], P(('groups', 'seq')), parts along dimension 0
The draws below stay inside these ranges and needn't reach their ends.
There are 2 independent parts, one for each index of `groups`. The reference program is written for one: setup_inputs(seed, part) draws one part's arguments, and reference() takes and returns one part's arrays. A program takes and returns all parts, laid end to end along the dimension named above; an argument that names none is the same for every part. Nothing has to cross between parts.
Inputs may be any that keep to these rules, and one draw needn't show every extreme that they name: `acceptor_shard`: in each device's list (aligned blocks of 256 junctions), at most 32 junctions name any one shard.
All inputs are finite; a program needn't handle non-finite values.
Results may differ from the reference program's by a relative error of at most 0.0059.
Values may be sent and summed in bfloat16 or wider, within the bound.
A program may use at most 64 MiB of HBM per device.

```python
import math
import jax
import jax.numpy as jnp
import numpy as np
from jax import lax

CHANNELS = 768
PAIR_WIDTH = 768
TRACKS = 256
TAPS = 5
ROWS_DEV = 512
JUNCTION_DEV = 256
LENGTH = 8192
JUNCTIONS = 4096
CAPACITY = 32
N_SEQ = 16


def draw_features(key, part):
    noise_key, row_key, column_key = jax.random.split(jax.random.fold_in(key, 17), 3)
    base_values = jnp.clip(jax.random.normal(noise_key, (LENGTH, CHANNELS), jnp.float32), -6.0, 6.0)
    row_scale = jnp.exp(jax.random.uniform(row_key, (LENGTH, 1), jnp.float32, math.log(0.3), math.log(3.0)))
    column_scale = jnp.exp(jax.random.uniform(column_key, (1, CHANNELS), jnp.float32, math.log(0.3), math.log(3.0)))
    return (base_values * row_scale * column_scale).astype(jnp.bfloat16)


def set_ends(array, stream_key, smallest, largest):
    longest = array.shape.index(max(array.shape))
    spots = []
    for shift in (0, 1):
        where = [jax.random.randint(jax.random.fold_in(stream_key, axis), (), 0, length) for axis, length in enumerate(array.shape)]
        where[longest] = (where[longest] + shift) % array.shape[longest]
        spots.append(tuple(where))
    return array.at[spots[0]].set(smallest).at[spots[1]].set(largest)


def level_of(rng, shape, shards, least, top_value):
    factor_of = 1.0
    for axis_at, blocks in shards:
        heights = jax.random.uniform(jax.random.fold_in(jax.random.fold_in(rng, 6), axis_at), (blocks,), jnp.float32, least / len(shards), top_value / len(shards))
        factor_of = factor_of * jnp.repeat(jnp.exp(heights), shape[axis_at] // blocks).reshape((-1,) + (1,) * (len(shape) - 1 - axis_at))
    return factor_of


def shared_out(rng, own, number, rows, count, top, limit, lean):
    order = jax.random.permutation(rng, count)
    crowded, ordinary = load_shares(count, rows * top, limit, lean, True), load_shares(count, rows * top, limit, lean, False)
    places = jnp.arange(count)

    def named(sizes, rotation):
        used = int((sizes > 0).sum())
        fixed = max(1, used // 4)
        shifted = fixed + (places - fixed + rotation * (used - fixed)) % max(1, count - fixed)
        return jnp.zeros((count,), jnp.int32).at[order[jnp.where(places < fixed, places, shifted)]].set(jnp.asarray(sizes, jnp.int32))

    sizes = jnp.where(number % 4 == 0, named(crowded, number // 4), named(ordinary, number - number // 4 - 1))
    mixed = jax.random.permutation(jax.random.fold_in(own, 3), count)
    donor, receiver = mixed[0:count // 2 * 2:2], mixed[1:count // 2 * 2:2]
    margin = jnp.minimum(sizes[donor] - 1, limit - sizes[receiver]) // 2
    margin = jnp.where((donor == order[0]) | (receiver == order[0]) | (sizes[receiver] == 0), 0, jnp.maximum(margin, 0))
    shifted = jax.random.randint(jax.random.fold_in(own, 4), (count // 2,), 0, 1 << 20) % (margin + 1)
    sizes = sizes.at[donor].add(-shifted).at[receiver].add(shifted)
    items = jnp.searchsorted(jnp.cumsum(sizes), jnp.arange(rows * top), side="right").astype(jnp.int32)
    table = items.reshape(top, rows).T
    table = table[jax.random.permutation(jax.random.fold_in(own, 1), rows)]
    rotation = jax.random.randint(jax.random.fold_in(own, 2), (rows, 1), 0, top)
    return jnp.take_along_axis(table, (jnp.arange(top)[None, :] + rotation) % top, axis=1)


def load_shares(number_of, total, limit, lean, full):
    loads = [(1 << 20) // math.isqrt(rank ** lean) + 1 for rank in range(1, number_of + 1)]
    largest = limit if full else min(limit, max(-(-total // number_of), total * loads[0] // sum(loads)))
    least = 1 if total - largest >= number_of - 1 else 0
    holding, spare = [largest] + [least] * (number_of - 1), total - largest - least * (number_of - 1)
    while spare > 0:
        free = [i for i in range(1, number_of) if holding[i] < largest] or [i for i in range(1, number_of) if holding[i] < limit]
        mass, remaining = sum([loads[i] for i in free]), spare
        for i in free:
            addition = min(limit - holding[i], max(1, remaining * loads[i] // mass), spare)
            holding[i] = holding[i] + addition
            spare = spare - addition
    return np.array(holding)


def centred(stream_key, extent, spread, reach, shards=(), kind=jnp.bfloat16):
    factor_of = level_of(stream_key, extent, shards, -0.22, 0.18) if shards else 1.0
    drawn = jax.random.normal(stream_key, extent, jnp.float32) * spread * factor_of
    return jnp.minimum(jnp.maximum(drawn, -reach), reach).astype(kind)


def setup_inputs(seed: int = 0, part: int = 0) -> dict:
    splits = jax.random.split(jax.random.key(seed), 13)
    part_keys = jax.random.split(jax.random.fold_in(splits[12], part), 13)
    features = draw_features(jax.random.fold_in(jax.random.fold_in(splits[12], part), 71), part)
    bases = set_ends(jax.random.randint(part_keys[1], (LENGTH,), 0, 4), jax.random.fold_in(part_keys[1], 1), 0, 3).astype(jnp.int32)
    base_table = centred(splits[2], (4, CHANNELS), 0.5, 3.0)
    norm_gain = jnp.clip(1.0 + 0.15 * jax.random.normal(splits[3], (CHANNELS,), jnp.float32), 0.25, 1.75).astype(jnp.bfloat16)
    conv_weight = centred(splits[4], (TAPS, CHANNELS, CHANNELS), (TAPS * CHANNELS) ** -0.5, 0.09375)
    donor_proj = centred(splits[5], (CHANNELS, PAIR_WIDTH), CHANNELS ** -0.5, 0.21875)
    acceptor_proj = centred(splits[6], (CHANNELS, PAIR_WIDTH), CHANNELS ** -0.5, 0.21875)
    track_weight = centred(splits[7], (TRACKS, PAIR_WIDTH), TRACKS ** -0.5, 0.375)
    donor_offset = set_ends(jax.random.randint(part_keys[8], (JUNCTIONS,), 0, ROWS_DEV), jax.random.fold_in(part_keys[8], 1), 0, ROWS_DEV - 1).astype(jnp.int32)
    acceptor_shard_keys = jax.random.split(jax.random.fold_in(part_keys[9], 1), JUNCTIONS // JUNCTION_DEV)
    acceptor_shard_turns = jax.random.permutation(jax.random.fold_in(part_keys[9], 3), JUNCTIONS // JUNCTION_DEV)
    acceptor_shard = jax.vmap(lambda own, number: shared_out(jax.random.fold_in(part_keys[9], 2), own, number, JUNCTION_DEV, N_SEQ, 1, CAPACITY, 2))(acceptor_shard_keys, acceptor_shard_turns).reshape((JUNCTIONS, 1))
    acceptor_offset = set_ends(jax.random.randint(part_keys[10], (JUNCTIONS,), 0, ROWS_DEV), jax.random.fold_in(part_keys[10], 1), 0, ROWS_DEV - 1).astype(jnp.int32)
    junction_cotangent = centred(part_keys[11], (JUNCTIONS, TRACKS), 1.0, 6.0, ((0, 16),))
    return dict(features=features, bases=bases, base_table=base_table, norm_gain=norm_gain, conv_weight=conv_weight, donor_proj=donor_proj, acceptor_proj=acceptor_proj, track_weight=track_weight, donor_offset=donor_offset, acceptor_shard=acceptor_shard, acceptor_offset=acceptor_offset, junction_cotangent=junction_cotangent)


def reference(features, bases, base_table, norm_gain, conv_weight, donor_proj, acceptor_proj, track_weight, donor_offset, acceptor_shard, acceptor_offset, junction_cotangent):
    embedded = features.astype(jnp.float32) + base_table.astype(jnp.float32)[bases]
    square_mean = lax.optimization_barrier(jnp.mean(embedded * embedded, axis=1, keepdims=True))
    normed = (embedded * lax.rsqrt(square_mean + 1e-06) * norm_gain.astype(jnp.float32)[None, :]).astype(jnp.bfloat16)
    padded = jnp.pad(normed, ((2, 2), (0, 0)))
    conv_out = jnp.zeros(embedded.shape, jnp.float32)
    for position in range(TAPS):
        conv_out = conv_out + jnp.dot(padded[position:position + LENGTH], conv_weight[position], preferred_element_type=jnp.float32)
    block_out = (embedded + jax.nn.gelu(conv_out, approximate=False)).astype(jnp.bfloat16)
    donor_emb = jnp.dot(block_out, donor_proj, preferred_element_type=jnp.float32).astype(jnp.bfloat16)
    acceptor_emb = jnp.dot(block_out, acceptor_proj, preferred_element_type=jnp.float32).astype(jnp.bfloat16)
    junction_ids = jnp.arange(JUNCTIONS, dtype=jnp.int32)
    donor_pos = junction_ids // JUNCTION_DEV * ROWS_DEV + donor_offset
    acceptor_pos = acceptor_shard[:, 0] * ROWS_DEV + acceptor_offset
    coefficient = jnp.dot(junction_cotangent, track_weight, preferred_element_type=jnp.float32)
    acceptor_grad = (coefficient * donor_emb[donor_pos].astype(jnp.float32)).astype(jnp.bfloat16)
    donor_grad = (coefficient * acceptor_emb[acceptor_pos].astype(jnp.float32)).astype(jnp.bfloat16)
    head_grad = jnp.zeros((LENGTH, CHANNELS), jnp.float32)
    head_grad = head_grad.at[donor_pos].add(jnp.dot(donor_grad, donor_proj.T, preferred_element_type=jnp.float32))
    head_grad = head_grad.at[acceptor_pos].add(jnp.dot(acceptor_grad, acceptor_proj.T, preferred_element_type=jnp.float32))
    return (block_out, head_grad)
```

```python
import functools

import jax
import jax.numpy as jnp
from jax import lax
from jax.experimental import pallas as pl
from jax.experimental.pallas import tpu as pltpu
from jax.sharding import PartitionSpec as P

F32 = jnp.float32
BF16 = jnp.bfloat16
I32 = jnp.int32
EDGE = 8


def iota(shape, dim):
    return lax.broadcasted_iota(I32, shape, dim)


def to_column(row):
    size = row.shape[1]
    eye = iota((size, size), 0) == iota((size, size), 1)
    return jnp.sum(jnp.where(eye, row, 0), axis=1, keepdims=True)


def dot(a, b):
    return jnp.dot(a, b, preferred_element_type=F32)


def dot_t(a, b):
    return lax.dot_general(a, b, (((1,), (1,)), ((), ())), preferred_element_type=F32)


def kernel(
    n,
    cap,
    feat_ref,
    bases_ref,
    table_ref,
    gain_ref,
    conv_hbm,
    donor_hbm,
    acceptor_hbm,
    track_ref,
    doff_ref,
    owner_ref,
    aoff_ref,
    cot_ref,
    block_ref,
    head_ref,
    npad,
    emb,
    xcol,
    conv_w,
    donor_w,
    acceptor_w,
    demb,
    aemb,
    coef,
    send_a,
    recv_a,
    send_b,
    recv_b,
    offs_send,
    offs_recv,
    doff_col,
    doff_row,
    aoff_col,
    scat_a,
    scat_d,
    local_sem,
    halo_send,
    halo_recv,
    offs_ssem,
    offs_rsem,
    a_ssem,
    a_rsem,
    b_ssem,
    b_rsem,
):
    rows, channels = feat_ref.shape
    taps = conv_hbm.shape[0]
    juncs = cot_ref.shape[0]
    slots = n * cap
    tile = min(slots, 512)
    tiles = slots // tile
    me = lax.axis_index("seq")
    right = lax.rem(me + 1, n)
    left = lax.rem(me + n - 1, n)

    copies = [
        pltpu.make_async_copy(
            conv_hbm.at[t], conv_w.at[pl.ds(t * channels, channels)], local_sem.at[t]
        )
        for t in range(taps)
    ]
    copies.append(pltpu.make_async_copy(donor_hbm, donor_w, local_sem.at[taps]))
    copies.append(pltpu.make_async_copy(acceptor_hbm, acceptor_w, local_sem.at[taps + 1]))
    for copy in copies:
        copy.start()

    def partner(i):
        sign = 1 - 2 * lax.rem(i, 2)
        return lax.rem(me + n // 2 + sign * ((i + 1) // 2), n)

    barrier = pltpu.get_barrier_semaphore()

    @pl.loop(0, n - 1)
    def _(i):
        pl.semaphore_signal(barrier, inc=1, device_id={"seq": partner(i)})

    letters = to_column(bases_ref[...])
    table = table_ref[...].astype(F32)
    base = jnp.where(
        letters == 0,
        table[0:1],
        jnp.where(letters == 1, table[1:2], jnp.where(letters == 2, table[2:3], table[3:4])),
    )
    embedded = feat_ref[...].astype(F32) + base
    emb[...] = embedded
    scale = lax.rsqrt(jnp.mean(embedded * embedded, axis=1, keepdims=True) + 1e-06)
    normed = (embedded * scale * gain_ref[...].astype(F32)).astype(BF16)
    npad[pl.ds(EDGE, rows)] = normed.astype(F32)

    owner_row = owner_ref[...]
    owner_col = to_column(owner_row)
    earlier = iota((juncs, juncs), 0) < iota((juncs, juncs), 1)
    same = owner_col == owner_row
    rank_row = jnp.sum(jnp.where(same & earlier, 1, 0), axis=0, keepdims=True)
    rank_col = to_column(rank_row)
    slot_row = owner_row * cap + rank_row
    slot_col = owner_col * cap + rank_col
    aoff_by_rank = jnp.where(rank_col == iota((juncs, 128), 1), to_column(aoff_ref[...]), 0)

    @pl.loop(0, n)
    def _(p):
        row = jnp.sum(jnp.where(owner_col == p, aoff_by_rank, 0), axis=0, keepdims=True)
        offs_send[p] = jnp.broadcast_to(row, (8, 128))

    pl.semaphore_wait(barrier, n - 1)

    halo_right = pltpu.make_async_remote_copy(
        src_ref=npad.at[pl.ds(rows, EDGE)],
        dst_ref=npad.at[pl.ds(0, EDGE)],
        send_sem=halo_send.at[0],
        recv_sem=halo_recv.at[0],
        device_id={"seq": right},
    )
    halo_left = pltpu.make_async_remote_copy(
        src_ref=npad.at[pl.ds(EDGE, EDGE)],
        dst_ref=npad.at[pl.ds(EDGE + rows, EDGE)],
        send_sem=halo_send.at[1],
        recv_sem=halo_recv.at[1],
        device_id={"seq": left},
    )
    halo_right.start()
    halo_left.start()

    def offs_copy(p, slot):
        return pltpu.make_async_remote_copy(
            src_ref=offs_send.at[p],
            dst_ref=offs_recv.at[slot],
            send_sem=offs_ssem.at[p],
            recv_sem=offs_rsem.at[slot],
            device_id={"seq": p},
        )

    def rows_copy(src, dst, ssem, rsem, p, slot):
        return pltpu.make_async_remote_copy(
            src_ref=src.at[pl.ds(pl.multiple_of(p * cap, cap), cap)],
            dst_ref=dst.at[pl.ds(pl.multiple_of(slot * cap, cap), cap)],
            send_sem=ssem.at[p],
            recv_sem=rsem.at[slot],
            device_id={"seq": p},
        )

    @pl.loop(0, n - 1)
    def _(i):
        offs_copy(partner(i), me).start()

    donor_col = to_column(doff_ref[...])

    @pl.loop(0, tiles)
    def _(k):
        at = pl.ds(pl.multiple_of(k * tile, tile), tile)
        hit = (iota((tile, juncs), 0) + k * tile) == slot_row
        doff_col[at] = jnp.broadcast_to(
            jnp.sum(jnp.where(hit, doff_ref[...], 0), axis=1, keepdims=True), (tile, 128)
        )
        hit_t = slot_col == (iota((juncs, tile), 1) + k * tile)
        doff_row[k] = jnp.broadcast_to(
            jnp.sum(jnp.where(hit_t, donor_col, 0), axis=0, keepdims=True), (8, tile)
        )
        picked = dot(jnp.where(hit, 1.0, 0.0).astype(BF16), cot_ref[...]).astype(BF16)
        coef[at] = dot(picked, track_ref[...])

    halo_right.wait()
    halo_left.wait()

    @pl.when(me == 0)
    def _():
        npad[pl.ds(0, EDGE)] = jnp.zeros((EDGE, channels), F32)

    @pl.when(me == n - 1)
    def _():
        npad[pl.ds(EDGE + rows, EDGE)] = jnp.zeros((EDGE, channels), F32)

    for t in range(taps):
        xcol[:, pl.ds(t * channels, channels)] = npad[
            pl.ds(EDGE - taps // 2 + t, rows)
        ].astype(BF16)
    for copy in copies:
        copy.wait()

    @pl.loop(0, channels // 256)
    def _(c):
        cols = pl.ds(pl.multiple_of(c * 256, 256), 256)
        out = dot(xcol[...], conv_w[:, cols])
        act = 0.5 * out * (1.0 + lax.erf(out * (0.5**0.5)))
        block_ref[:, cols] = (emb[:, cols] + act).astype(BF16)

    demb[...] = dot(block_ref[...], donor_w[...]).astype(BF16)

    @pl.loop(0, tiles)
    def _(k):
        at = pl.ds(pl.multiple_of(k * tile, tile), tile)
        pick = jnp.where(doff_col[at][:, 0:1] == iota((tile, rows), 1), 1.0, 0.0).astype(BF16)
        send_a[at] = (coef[at] * dot(pick, demb[...])).astype(BF16)

    @pl.loop(0, n - 1)
    def _(i):
        rows_copy(send_a, recv_a, a_ssem, a_rsem, partner(i), me).start()

    aemb[...] = dot(block_ref[...], acceptor_w[...]).astype(BF16)

    @pl.loop(0, n - 1)
    def _(i):
        p = partner(i)
        offs_copy(p, me).wait_send()
        offs_copy(p, p).wait_recv()

    offs_recv[me] = offs_send[me]

    @pl.loop(0, n)
    def _(p):
        row = offs_recv[p][0:1]
        mask = iota((cap, 128), 0) == iota((cap, 128), 1)
        aoff_col[pl.ds(pl.multiple_of(p * cap, cap), cap)] = jnp.broadcast_to(
            jnp.sum(jnp.where(mask, row, 0), axis=1, keepdims=True), (cap, 128)
        )

    @pl.loop(0, tiles)
    def _(k):
        at = pl.ds(pl.multiple_of(k * tile, tile), tile)
        pick = jnp.where(aoff_col[at][:, 0:1] == iota((tile, rows), 1), 1.0, 0.0).astype(BF16)
        send_b[at] = dot(pick, aemb[...]).astype(BF16)

    @pl.loop(0, n - 1)
    def _(i):
        rows_copy(send_b, recv_b, b_ssem, b_rsem, partner(i), me).start()

    own = pl.ds(pl.multiple_of(me * cap, cap), cap)
    recv_a[own] = send_a[own]
    recv_b[own] = send_b[own]
    scat_a[...] = jnp.zeros_like(scat_a)
    scat_d[...] = jnp.zeros_like(scat_d)

    @pl.loop(0, n - 1)
    def _(i):
        p = partner(i)
        rows_copy(send_a, recv_a, a_ssem, a_rsem, p, p).wait_recv()

    @pl.loop(0, tiles)
    def _(k):
        at = pl.ds(pl.multiple_of(k * tile, tile), tile)
        eye = iota((tile, tile), 0) == iota((tile, tile), 1)
        where = jnp.sum(jnp.where(eye, aoff_col[at][:, 0:1], 0), axis=0, keepdims=True)
        put = jnp.where(iota((rows, tile), 0) == where, 1.0, 0.0).astype(BF16)
        scat_a[...] += dot(put, recv_a[at])

    head_ref[...] = dot_t(scat_a[...].astype(BF16), acceptor_w[...])

    @pl.loop(0, n - 1)
    def _(i):
        p = partner(i)
        rows_copy(send_b, recv_b, b_ssem, b_rsem, p, p).wait_recv()

    @pl.loop(0, tiles)
    def _(k):
        at = pl.ds(pl.multiple_of(k * tile, tile), tile)
        grad = (coef[at] * recv_b[at].astype(F32)).astype(BF16)
        put = jnp.where(iota((rows, tile), 0) == doff_row[k][0:1], 1.0, 0.0).astype(BF16)
        scat_d[...] += dot(put, grad)

    head_ref[...] += dot_t(scat_d[...].astype(BF16), donor_w[...])

    @pl.loop(0, n - 1)
    def _(i):
        p = partner(i)
        rows_copy(send_a, recv_a, a_ssem, a_rsem, p, me).wait_send()
        rows_copy(send_b, recv_b, b_ssem, b_rsem, p, me).wait_send()


def on_device(
    features,
    bases,
    base_table,
    norm_gain,
    conv_weight,
    donor_proj,
    acceptor_proj,
    track_weight,
    donor_offset,
    acceptor_shard,
    acceptor_offset,
    junction_cotangent,
):
    n = lax.axis_size("seq")
    rows, channels = features.shape
    taps = conv_weight.shape[0]
    pair = donor_proj.shape[1]
    juncs = donor_offset.shape[0]
    cap = max(2 * juncs // n, 16)
    slots = n * cap
    tile = min(slots, 512)
    vmem = pl.BlockSpec(memory_space=pltpu.VMEM)
    hbm = pl.BlockSpec(memory_space=pl.ANY)
    dma = pltpu.SemaphoreType.DMA
    return pl.pallas_call(
        functools.partial(kernel, n, cap),
        out_shape=(
            jax.ShapeDtypeStruct((rows, channels), BF16),
            jax.ShapeDtypeStruct((rows, channels), F32),
        ),
        in_specs=[vmem, vmem, vmem, vmem, hbm, hbm, hbm, vmem, vmem, vmem, vmem, vmem],
        out_specs=(vmem, vmem),
        scratch_shapes=[
            pltpu.VMEM((rows + 2 * EDGE, channels), F32),
            pltpu.VMEM((rows, channels), F32),
            pltpu.VMEM((rows, taps * channels), BF16),
            pltpu.VMEM((taps * channels, channels), BF16),
            pltpu.VMEM((channels, pair), BF16),
            pltpu.VMEM((channels, pair), BF16),
            pltpu.VMEM((rows, pair), BF16),
            pltpu.VMEM((rows, pair), BF16),
            pltpu.VMEM((slots, pair), F32),
            pltpu.VMEM((slots, pair), BF16),
            pltpu.VMEM((slots, pair), BF16),
            pltpu.VMEM((slots, pair), BF16),
            pltpu.VMEM((slots, pair), BF16),
            pltpu.VMEM((n, 8, 128), I32),
            pltpu.VMEM((n, 8, 128), I32),
            pltpu.VMEM((slots, 128), I32),
            pltpu.VMEM((slots // tile, 8, tile), I32),
            pltpu.VMEM((slots, 128), I32),
            pltpu.VMEM((rows, pair), F32),
            pltpu.VMEM((rows, pair), F32),
            dma((taps + 2,)),
            dma((2,)),
            dma((2,)),
            dma((n,)),
            dma((n,)),
            dma((n,)),
            dma((n,)),
            dma((n,)),
            dma((n,)),
        ],
        compiler_params=pltpu.CompilerParams(
            collective_id=0, has_side_effects=True, vmem_limit_bytes=58 * 1024 * 1024
        ),
        name="block_and_pairs",
    )(
        features,
        bases.reshape(1, rows),
        base_table,
        norm_gain.reshape(1, channels),
        conv_weight,
        donor_proj,
        acceptor_proj,
        track_weight,
        donor_offset.reshape(1, juncs),
        acceptor_shard.reshape(1, juncs),
        acceptor_offset.reshape(1, juncs),
        junction_cotangent,
    )


def solution(mesh):
    split = ("groups", "seq")
    in_specs = (
        P(split, None),
        P(split),
        P(),
        P(),
        P(),
        P(),
        P(),
        P(),
        P(split),
        P(split, None),
        P(split),
        P(split, None),
    )
    out_specs = (P(split, None), P(split, None))
    return jax.shard_map(
        on_device, mesh=mesh, in_specs=in_specs, out_specs=out_specs, check_vma=False
    )
```

```python
import functools

import jax
import jax.numpy as jnp
from jax import lax
from jax.experimental import pallas as pl
from jax.experimental.pallas import tpu as pltpu
from jax.sharding import PartitionSpec as P

F32 = jnp.float32
BF16 = jnp.bfloat16
I32 = jnp.int32
EDGE = 8
WIDE = 256


def iota(shape, dim):
    return lax.broadcasted_iota(I32, shape, dim)


def to_column(row):
    size = row.shape[1]
    eye = iota((size, size), 0) == iota((size, size), 1)
    return jnp.sum(jnp.where(eye, row, 0), axis=1, keepdims=True)


def dot(a, b):
    return jnp.dot(a, b, preferred_element_type=F32)


def dot_t(a, b):
    return lax.dot_general(a, b, (((1,), (1,)), ((), ())), preferred_element_type=F32)


def kernel(
    n,
    cap,
    feat_ref,
    bases_ref,
    table_ref,
    gain_ref,
    conv_hbm,
    donor_hbm,
    acceptor_hbm,
    track_ref,
    doff_ref,
    owner_ref,
    aoff_ref,
    cot_ref,
    block_hbm,
    head_hbm,
    scat_hbm,
    npad,
    emb,
    xcol,
    conv_w,
    donor_w,
    acceptor_w,
    demb,
    aemb,
    coef,
    send_a,
    recv_a,
    send_b,
    recv_b,
    offs_send,
    offs_recv,
    doff_col,
    doff_row,
    aoff_col,
    scat_a,
    scat_d,
    pick_b,
    put_a,
    block_ref,
    head_ref,
    scat_out,
    local_sem,
    out_sem,
    halo_send,
    halo_recv,
    offs_ssem,
    offs_rsem,
    a_ssem,
    a_rsem,
    b_ssem,
    b_rsem,
):
    rows, channels = feat_ref.shape
    taps = conv_hbm.shape[0]
    juncs = cot_ref.shape[0]
    slots = n * cap
    tile = min(slots, 512)
    tiles = slots // tile
    chunks = donor_hbm.shape[1] // WIDE
    me = lax.axis_index("seq")
    right = lax.rem(me + 1, n)
    left = lax.rem(me + n - 1, n)

    copies = [
        pltpu.make_async_copy(
            conv_hbm.at[t], conv_w.at[pl.ds(t * channels, channels)], local_sem.at[t]
        )
        for t in range(taps)
    ]
    copies.append(pltpu.make_async_copy(donor_hbm, donor_w, local_sem.at[taps]))
    copies.append(pltpu.make_async_copy(acceptor_hbm, acceptor_w, local_sem.at[taps + 1]))
    for copy in copies:
        copy.start()

    def partner(i):
        sign = 1 - 2 * lax.rem(i, 2)
        return lax.rem(me + n // 2 + sign * ((i + 1) // 2), n)

    barrier = pltpu.get_barrier_semaphore()

    @pl.loop(0, n - 1)
    def _(i):
        pl.semaphore_signal(barrier, inc=1, device_id={"seq": partner(i)})

    letters = to_column(bases_ref[...])
    table = table_ref[...].astype(F32)
    base = jnp.where(
        letters == 0,
        table[0:1],
        jnp.where(letters == 1, table[1:2], jnp.where(letters == 2, table[2:3], table[3:4])),
    )
    embedded = feat_ref[...].astype(F32) + base
    emb[...] = embedded
    scale = lax.rsqrt(jnp.mean(embedded * embedded, axis=1, keepdims=True) + 1e-06)
    normed = (embedded * scale * gain_ref[...].astype(F32)[None, :]).astype(BF16)
    npad[pl.ds(EDGE, rows)] = normed.astype(F32)

    owner_row = owner_ref[...]
    owner_col = to_column(owner_row)
    earlier = iota((juncs, juncs), 0) < iota((juncs, juncs), 1)
    same = owner_col == owner_row
    rank_row = jnp.sum(jnp.where(same & earlier, 1, 0), axis=0, keepdims=True)
    rank_col = to_column(rank_row)
    slot_row = owner_row * cap + rank_row
    slot_col = owner_col * cap + rank_col
    aoff_by_rank = jnp.where(rank_col == iota((juncs, 128), 1), to_column(aoff_ref[...]), 0)

    @pl.loop(0, n)
    def _(p):
        row = jnp.sum(jnp.where(owner_col == p, aoff_by_rank, 0), axis=0, keepdims=True)
        offs_send[p] = jnp.broadcast_to(row, (8, 128))

    pl.semaphore_wait(barrier, n - 1)

    halo_right = pltpu.make_async_remote_copy(
        src_ref=npad.at[pl.ds(rows, EDGE)],
        dst_ref=npad.at[pl.ds(0, EDGE)],
        send_sem=halo_send.at[0],
        recv_sem=halo_recv.at[0],
        device_id={"seq": right},
    )
    halo_left = pltpu.make_async_remote_copy(
        src_ref=npad.at[pl.ds(EDGE, EDGE)],
        dst_ref=npad.at[pl.ds(EDGE + rows, EDGE)],
        send_sem=halo_send.at[1],
        recv_sem=halo_recv.at[1],
        device_id={"seq": left},
    )
    halo_right.start()
    halo_left.start()

    def offs_copy(p, slot):
        return pltpu.make_async_remote_copy(
            src_ref=offs_send.at[p],
            dst_ref=offs_recv.at[slot],
            send_sem=offs_ssem.at[p],
            recv_sem=offs_rsem.at[slot],
            device_id={"seq": p},
        )

    def rows_copy(src, dst, ssem, rsem, c, p, slot):
        cols = pl.ds(c * WIDE, WIDE)
        return pltpu.make_async_remote_copy(
            src_ref=src.at[pl.ds(pl.multiple_of(p * cap, cap), cap), cols],
            dst_ref=dst.at[pl.ds(pl.multiple_of(slot * cap, cap), cap), cols],
            send_sem=ssem.at[c, p],
            recv_sem=rsem.at[c, slot],
            device_id={"seq": p},
        )

    @pl.loop(0, n - 1)
    def _(i):
        offs_copy(partner(i), me).start()

    halo_right.wait()
    halo_left.wait()

    @pl.when(me == 0)
    def _():
        npad[pl.ds(0, EDGE)] = jnp.zeros((EDGE, channels), F32)

    @pl.when(me == n - 1)
    def _():
        npad[pl.ds(EDGE + rows, EDGE)] = jnp.zeros((EDGE, channels), F32)

    for t in range(taps):
        xcol[:, pl.ds(t * channels, channels)] = npad[
            pl.ds(EDGE - taps // 2 + t, rows)
        ].astype(BF16)

    @pl.loop(0, n - 1)
    def _(i):
        p = partner(i)
        offs_copy(p, me).wait_send()
        offs_copy(p, p).wait_recv()

    offs_recv[me] = offs_send[me]

    @pl.loop(0, n)
    def _(p):
        row = offs_recv[p][0:1]
        mask = iota((cap, 128), 0) == iota((cap, 128), 1)
        aoff_col[pl.ds(pl.multiple_of(p * cap, cap), cap)] = jnp.broadcast_to(
            jnp.sum(jnp.where(mask, row, 0), axis=1, keepdims=True), (cap, 128)
        )

    @pl.loop(0, tiles)
    def _(k):
        at = pl.ds(pl.multiple_of(k * tile, tile), tile)
        hit = aoff_col[at][:, 0:1] == iota((tile, rows), 1)
        pick_b[at] = jnp.where(hit, 1.0, 0.0).astype(BF16)

    for copy in copies:
        copy.wait()

    for c in range(channels // WIDE):
        cols = pl.ds(c * WIDE, WIDE)
        out = dot(xcol[...], conv_w[:, cols])
        act = 0.5 * out * (1.0 + lax.erf(out * (0.5**0.5)))
        block_ref[:, cols] = (emb[:, cols] + act).astype(BF16)

    for c in range(chunks):
        cols = pl.ds(c * WIDE, WIDE)
        aemb[...] = dot(block_ref[...], acceptor_w[:, cols]).astype(BF16)

        @pl.loop(0, tiles)
        def _(k):
            at = pl.ds(pl.multiple_of(k * tile, tile), tile)
            send_b[at, cols] = dot(pick_b[at], aemb[...]).astype(BF16)

        @pl.loop(0, n - 1)
        def _(i):
            rows_copy(send_b, recv_b, b_ssem, b_rsem, c, partner(i), me).start()

    block_out = pltpu.make_async_copy(block_ref, block_hbm, out_sem.at[0])
    block_out.start()
    donor_col = to_column(doff_ref[...])

    @pl.loop(0, tiles)
    def _(k):
        at = pl.ds(pl.multiple_of(k * tile, tile), tile)
        hit = (iota((tile, juncs), 0) + k * tile) == slot_row
        doff_col[at] = jnp.broadcast_to(
            jnp.sum(jnp.where(hit, doff_ref[...], 0), axis=1, keepdims=True), (tile, 128)
        )
        hit_t = slot_col == (iota((juncs, tile), 1) + k * tile)
        doff_row[k] = jnp.broadcast_to(
            jnp.sum(jnp.where(hit_t, donor_col, 0), axis=0, keepdims=True), (8, tile)
        )
        picked = dot(jnp.where(hit, 1.0, 0.0).astype(BF16), cot_ref[...]).astype(BF16)
        coef[at] = dot(picked, track_ref[...])

    demb[...] = dot(block_ref[...], donor_w[...]).astype(BF16)

    @pl.loop(0, tiles)
    def _(k):
        at = pl.ds(pl.multiple_of(k * tile, tile), tile)
        pick = jnp.where(doff_col[at][:, 0:1] == iota((tile, rows), 1), 1.0, 0.0).astype(BF16)
        send_a[at] = (coef[at] * dot(pick, demb[...])).astype(BF16)

    for c in range(chunks):

        @pl.loop(0, n - 1)
        def _(i):
            rows_copy(send_a, recv_a, a_ssem, a_rsem, c, partner(i), me).start()

    own = pl.ds(pl.multiple_of(me * cap, cap), cap)
    recv_a[own] = send_a[own]
    recv_b[own] = send_b[own]
    scat_a[...] = jnp.zeros_like(scat_a)
    scat_d[...] = jnp.zeros_like(scat_d)

    for c in range(chunks):

        @pl.loop(0, n - 1)
        def _(i):
            p = partner(i)
            rows_copy(send_b, recv_b, b_ssem, b_rsem, c, p, p).wait_recv()

    @pl.loop(0, tiles)
    def _(k):
        at = pl.ds(pl.multiple_of(k * tile, tile), tile)
        grad = (coef[at] * recv_b[at].astype(F32)).astype(BF16)
        put = jnp.where(iota((rows, tile), 0) == doff_row[k][0:1], 1.0, 0.0).astype(BF16)
        scat_d[...] += dot(put, grad)

    head_ref[...] = dot_t(scat_d[...].astype(BF16), donor_w[...])
    head_out = pltpu.make_async_copy(head_ref, head_hbm, out_sem.at[1])
    head_out.start()

    @pl.loop(0, tiles)
    def _(k):
        at = pl.ds(pl.multiple_of(k * tile, tile), tile)
        eye = iota((tile, tile), 0) == iota((tile, tile), 1)
        where = jnp.sum(jnp.where(eye, aoff_col[at][:, 0:1], 0), axis=0, keepdims=True)
        put = jnp.where(iota((rows, tile), 0) == where, 1.0, 0.0).astype(BF16)
        put_a[k] = put

    block_out.wait()
    head_out.wait()

    for c in range(chunks):

        @pl.loop(0, n - 1)
        def _(i):
            p = partner(i)
            rows_copy(send_b, recv_b, b_ssem, b_rsem, c, p, me).wait_send()
            rows_copy(send_a, recv_a, a_ssem, a_rsem, c, p, me).wait_send()
            rows_copy(send_a, recv_a, a_ssem, a_rsem, c, p, p).wait_recv()

    @pl.loop(0, tiles)
    def _(k):
        at = pl.ds(pl.multiple_of(k * tile, tile), tile)
        scat_a[...] += dot(put_a[k], recv_a[at])

    scat_out[...] = scat_a[...].astype(BF16)
    last = pltpu.make_async_copy(scat_out, scat_hbm, out_sem.at[2])
    last.start()
    last.wait()


def finish(block_ref, head_ref, scat_ref, proj_ref, block_out, head_out):
    block_out[...] = block_ref[...]
    head_out[...] = head_ref[...] + dot_t(scat_ref[...], proj_ref[...])


def on_device(
    features,
    bases,
    base_table,
    norm_gain,
    conv_weight,
    donor_proj,
    acceptor_proj,
    track_weight,
    donor_offset,
    acceptor_shard,
    acceptor_offset,
    junction_cotangent,
):
    n = lax.axis_size("seq")
    rows, channels = features.shape
    taps = conv_weight.shape[0]
    pair = donor_proj.shape[1]
    juncs = donor_offset.shape[0]
    cap = max(2 * juncs // n, 16)
    slots = n * cap
    tile = min(slots, 512)
    vmem = pl.BlockSpec(memory_space=pltpu.VMEM)
    hbm = pl.BlockSpec(memory_space=pl.ANY)
    dma = pltpu.SemaphoreType.DMA
    chunks = pair // WIDE
    block, head, scat = pl.pallas_call(
        functools.partial(kernel, n, cap),
        out_shape=(
            jax.ShapeDtypeStruct((rows, channels), BF16),
            jax.ShapeDtypeStruct((rows, channels), F32),
            jax.ShapeDtypeStruct((rows, pair), BF16),
        ),
        in_specs=[vmem, vmem, vmem, vmem, hbm, hbm, hbm, vmem, vmem, vmem, vmem, vmem],
        out_specs=(hbm, hbm, hbm),
        scratch_shapes=[
            pltpu.VMEM((rows + 2 * EDGE, channels), F32),
            pltpu.VMEM((rows, channels), F32),
            pltpu.VMEM((rows, taps * channels), BF16),
            pltpu.VMEM((taps * channels, channels), BF16),
            pltpu.VMEM((channels, pair), BF16),
            pltpu.VMEM((channels, pair), BF16),
            pltpu.VMEM((rows, pair), BF16),
            pltpu.VMEM((rows, WIDE), BF16),
            pltpu.VMEM((slots, pair), F32),
            pltpu.VMEM((slots, pair), BF16),
            pltpu.VMEM((slots, pair), BF16),
            pltpu.VMEM((slots, pair), BF16),
            pltpu.VMEM((slots, pair), BF16),
            pltpu.VMEM((n, 8, 128), I32),
            pltpu.VMEM((n, 8, 128), I32),
            pltpu.VMEM((slots, 128), I32),
            pltpu.VMEM((slots // tile, 8, tile), I32),
            pltpu.VMEM((slots, 128), I32),
            pltpu.VMEM((rows, pair), F32),
            pltpu.VMEM((rows, pair), F32),
            pltpu.VMEM((slots, rows), BF16),
            pltpu.VMEM((slots // tile, rows, tile), BF16),
            pltpu.VMEM((rows, channels), BF16),
            pltpu.VMEM((rows, channels), F32),
            pltpu.VMEM((rows, pair), BF16),
            dma((taps + 2,)),
            dma((3,)),
            dma((2,)),
            dma((2,)),
            dma((n,)),
            dma((n,)),
            dma((chunks, n)),
            dma((chunks, n)),
            dma((chunks, n)),
            dma((chunks, n)),
        ],
        compiler_params=pltpu.CompilerParams(
            collective_id=0, has_side_effects=True, vmem_limit_bytes=58 * 1024 * 1024
        ),
        name="block_and_pairs",
    )(
        features,
        bases.reshape(1, rows),
        base_table,
        norm_gain,
        conv_weight,
        donor_proj,
        acceptor_proj,
        track_weight,
        donor_offset.reshape(1, juncs),
        acceptor_shard.reshape(1, juncs),
        acceptor_offset.reshape(1, juncs),
        junction_cotangent,
    )
    step = min(rows, 128)
    line = pl.BlockSpec((step, channels), lambda i: (i, 0))
    return pl.pallas_call(
        finish,
        grid=(rows // step,),
        out_shape=(
            jax.ShapeDtypeStruct((rows, channels), BF16),
            jax.ShapeDtypeStruct((rows, channels), F32),
        ),
        in_specs=[
            line,
            line,
            pl.BlockSpec((step, pair), lambda i: (i, 0)),
            pl.BlockSpec((channels, pair), lambda i: (0, 0)),
        ],
        out_specs=(line, line),
        name="finish",
    )(block, head, scat, acceptor_proj)


def solution(mesh):
    split = ("groups", "seq")
    in_specs = (
        P(split, None),
        P(split),
        P(),
        P(),
        P(),
        P(),
        P(),
        P(),
        P(split),
        P(split, None),
        P(split),
        P(split, None),
    )
    out_specs = (P(split, None), P(split, None))
    return jax.shard_map(
        on_device, mesh=mesh, in_specs=in_specs, out_specs=out_specs, check_vma=False
    )
```

```python
import functools

import jax
import jax.numpy as jnp
from jax import lax
from jax.experimental import pallas as pl
from jax.experimental.pallas import tpu as pltpu
from jax.sharding import PartitionSpec as P

F32 = jnp.float32
BF16 = jnp.bfloat16
I32 = jnp.int32
EDGE = 8


def iota(shape, dim):
    return lax.broadcasted_iota(I32, shape, dim)


def to_column(row):
    size = row.shape[1]
    eye = iota((size, size), 0) == iota((size, size), 1)
    return jnp.sum(jnp.where(eye, row, 0), axis=1, keepdims=True)


def dot(a, b):
    return jnp.dot(a, b, preferred_element_type=F32)


def dot_t(a, b):
    return lax.dot_general(a, b, (((1,), (1,)), ((), ())), preferred_element_type=F32)


def kernel(
    n,
    cap,
    feat_ref,
    bases_ref,
    table_ref,
    gain_ref,
    conv_hbm,
    donor_hbm,
    acceptor_hbm,
    track_ref,
    doff_ref,
    owner_ref,
    aoff_ref,
    cot_ref,
    block_ref,
    head_ref,
    npad,
    emb,
    xcol,
    conv_w,
    donor_w,
    acceptor_w,
    demb,
    aemb,
    coef,
    send_a,
    recv_a,
    send_b,
    recv_b,
    offs_send,
    offs_recv,
    doff_col,
    doff_row,
    aoff_col,
    scat_a,
    scat_d,
    put_a,
    put_d,
    local_sem,
    halo_send,
    halo_recv,
    offs_ssem,
    offs_rsem,
    a_ssem,
    a_rsem,
    b_ssem,
    b_rsem,
):
    rows, channels = feat_ref.shape
    taps = conv_hbm.shape[0]
    juncs = cot_ref.shape[0]
    slots = n * cap
    tile = min(slots, 512)
    tiles = slots // tile
    me = lax.axis_index("seq")
    right = lax.rem(me + 1, n)
    left = lax.rem(me + n - 1, n)

    copies = [
        pltpu.make_async_copy(
            conv_hbm.at[t], conv_w.at[pl.ds(t * channels, channels)], local_sem.at[t]
        )
        for t in range(taps)
    ]
    copies.append(pltpu.make_async_copy(donor_hbm, donor_w, local_sem.at[taps]))
    copies.append(pltpu.make_async_copy(acceptor_hbm, acceptor_w, local_sem.at[taps + 1]))
    for copy in copies:
        copy.start()

    def partner(i):
        half = i // 2
        sign = 1 - 2 * lax.rem(half, 2)
        near = lax.rem(i, 2)
        step = (1 - near) * (n // 2) + sign * (1 - 2 * near) * ((half + 1) // 2 + near * (1 - lax.rem(half, 2)))
        return lax.rem(me + n + step, n)

    barrier = pltpu.get_barrier_semaphore()

    @pl.loop(0, n - 1)
    def _(i):
        pl.semaphore_signal(barrier, inc=1, device_id={"seq": partner(i)})

    letters = to_column(bases_ref[...])
    table = table_ref[...].astype(F32)
    base = jnp.where(
        letters == 0,
        table[0:1],
        jnp.where(letters == 1, table[1:2], jnp.where(letters == 2, table[2:3], table[3:4])),
    )
    embedded = feat_ref[...].astype(F32) + base
    emb[...] = embedded
    scale = lax.rsqrt(jnp.mean(embedded * embedded, axis=1, keepdims=True) + 1e-06)
    normed = (embedded * scale * gain_ref[...].astype(F32)[None, :]).astype(BF16)
    npad[pl.ds(EDGE, rows)] = normed.astype(F32)

    owner_row = owner_ref[...]
    owner_col = to_column(owner_row)
    earlier = iota((juncs, juncs), 0) < iota((juncs, juncs), 1)
    same = owner_col == owner_row
    rank_row = jnp.sum(jnp.where(same & earlier, 1, 0), axis=0, keepdims=True)
    rank_col = to_column(rank_row)
    slot_row = owner_row * cap + rank_row
    slot_col = owner_col * cap + rank_col
    aoff_by_rank = jnp.where(rank_col == iota((juncs, 128), 1), to_column(aoff_ref[...]), 0)

    @pl.loop(0, n)
    def _(p):
        row = jnp.sum(jnp.where(owner_col == p, aoff_by_rank, 0), axis=0, keepdims=True)
        offs_send[p] = jnp.broadcast_to(row, (8, 128))

    pl.semaphore_wait(barrier, n - 1)

    halo_right = pltpu.make_async_remote_copy(
        src_ref=npad.at[pl.ds(rows, EDGE)],
        dst_ref=npad.at[pl.ds(0, EDGE)],
        send_sem=halo_send.at[0],
        recv_sem=halo_recv.at[0],
        device_id={"seq": right},
    )
    halo_left = pltpu.make_async_remote_copy(
        src_ref=npad.at[pl.ds(EDGE, EDGE)],
        dst_ref=npad.at[pl.ds(EDGE + rows, EDGE)],
        send_sem=halo_send.at[1],
        recv_sem=halo_recv.at[1],
        device_id={"seq": left},
    )
    halo_right.start()
    halo_left.start()

    def offs_copy(p, slot):
        return pltpu.make_async_remote_copy(
            src_ref=offs_send.at[p],
            dst_ref=offs_recv.at[slot],
            send_sem=offs_ssem.at[p],
            recv_sem=offs_rsem.at[slot],
            device_id={"seq": p},
        )

    def rows_copy(src, dst, ssem, rsem, p, slot):
        return pltpu.make_async_remote_copy(
            src_ref=src.at[pl.ds(pl.multiple_of(p * cap, cap), cap)],
            dst_ref=dst.at[pl.ds(pl.multiple_of(slot * cap, cap), cap)],
            send_sem=ssem.at[p],
            recv_sem=rsem.at[slot],
            device_id={"seq": p},
        )

    @pl.loop(0, n - 1)
    def _(i):
        offs_copy(partner(i), me).start()

    donor_col = to_column(doff_ref[...])

    @pl.loop(0, tiles)
    def _(k):
        at = pl.ds(pl.multiple_of(k * tile, tile), tile)
        hit = (iota((tile, juncs), 0) + k * tile) == slot_row
        doff_col[at] = jnp.broadcast_to(
            jnp.sum(jnp.where(hit, doff_ref[...], 0), axis=1, keepdims=True), (tile, 128)
        )
        hit_t = slot_col == (iota((juncs, tile), 1) + k * tile)
        doff_row[k] = jnp.broadcast_to(
            jnp.sum(jnp.where(hit_t, donor_col, 0), axis=0, keepdims=True), (8, tile)
        )
        picked = dot(jnp.where(hit, 1.0, 0.0).astype(BF16), cot_ref[...]).astype(BF16)
        coef[at] = dot(picked, track_ref[...])

    halo_right.wait()
    halo_left.wait()

    @pl.when(me == 0)
    def _():
        npad[pl.ds(0, EDGE)] = jnp.zeros((EDGE, channels), F32)

    @pl.when(me == n - 1)
    def _():
        npad[pl.ds(EDGE + rows, EDGE)] = jnp.zeros((EDGE, channels), F32)

    for t in range(taps):
        xcol[:, pl.ds(t * channels, channels)] = npad[
            pl.ds(EDGE - taps // 2 + t, rows)
        ].astype(BF16)
    for copy in copies:
        copy.wait()

    @pl.loop(0, channels // 256)
    def _(c):
        cols = pl.ds(pl.multiple_of(c * 256, 256), 256)
        out = dot(xcol[...], conv_w[:, cols])
        act = 0.5 * out * (1.0 + lax.erf(out * (0.5**0.5)))
        block_ref[:, cols] = (emb[:, cols] + act).astype(BF16)

    demb[...] = dot(block_ref[...], donor_w[...]).astype(BF16)

    @pl.loop(0, tiles)
    def _(k):
        at = pl.ds(pl.multiple_of(k * tile, tile), tile)
        pick = jnp.where(doff_col[at][:, 0:1] == iota((tile, rows), 1), 1.0, 0.0).astype(BF16)
        send_a[at] = (coef[at] * dot(pick, demb[...])).astype(BF16)

    @pl.loop(0, n - 1)
    def _(i):
        rows_copy(send_a, recv_a, a_ssem, a_rsem, partner(i), me).start()

    aemb[...] = dot(block_ref[...], acceptor_w[...]).astype(BF16)

    @pl.loop(0, n - 1)
    def _(i):
        p = partner(i)
        offs_copy(p, me).wait_send()
        offs_copy(p, p).wait_recv()

    offs_recv[me] = offs_send[me]

    @pl.loop(0, n)
    def _(p):
        row = offs_recv[p][0:1]
        mask = iota((cap, 128), 0) == iota((cap, 128), 1)
        aoff_col[pl.ds(pl.multiple_of(p * cap, cap), cap)] = jnp.broadcast_to(
            jnp.sum(jnp.where(mask, row, 0), axis=1, keepdims=True), (cap, 128)
        )

    @pl.loop(0, tiles)
    def _(k):
        at = pl.ds(pl.multiple_of(k * tile, tile), tile)
        pick = jnp.where(aoff_col[at][:, 0:1] == iota((tile, rows), 1), 1.0, 0.0).astype(BF16)
        send_b[at] = dot(pick, aemb[...]).astype(BF16)

    @pl.loop(0, n - 1)
    def _(i):
        rows_copy(send_b, recv_b, b_ssem, b_rsem, partner(i), me).start()

    own = pl.ds(pl.multiple_of(me * cap, cap), cap)
    recv_a[own] = send_a[own]
    recv_b[own] = send_b[own]
    if tiles > 1:
        scat_a[...] = jnp.zeros_like(scat_a)
        scat_d[...] = jnp.zeros_like(scat_d)

    @pl.loop(0, tiles)
    def _(k):
        at = pl.ds(pl.multiple_of(k * tile, tile), tile)
        eye = iota((tile, tile), 0) == iota((tile, tile), 1)
        where = jnp.sum(jnp.where(eye, aoff_col[at][:, 0:1], 0), axis=0, keepdims=True)
        put_a[k] = jnp.where(iota((rows, tile), 0) == where, 1.0, 0.0).astype(BF16)
        put_d[k] = jnp.where(iota((rows, tile), 0) == doff_row[k][0:1], 1.0, 0.0).astype(BF16)

    def scatter(total, put, values):
        if tiles > 1:
            total[...] += dot(put, values)
        else:
            total[...] = dot(put, values)

    @pl.loop(0, n - 1)
    def _(i):
        p = partner(i)
        rows_copy(send_a, recv_a, a_ssem, a_rsem, p, p).wait_recv()

    @pl.loop(0, tiles)
    def _(k):
        at = pl.ds(pl.multiple_of(k * tile, tile), tile)
        scatter(scat_a, put_a[k], recv_a[at])

    head_ref[...] = dot_t(scat_a[...].astype(BF16), acceptor_w[...])

    @pl.loop(0, n - 1)
    def _(i):
        p = partner(i)
        rows_copy(send_b, recv_b, b_ssem, b_rsem, p, p).wait_recv()

    @pl.loop(0, tiles)
    def _(k):
        at = pl.ds(pl.multiple_of(k * tile, tile), tile)
        grad = (coef[at] * recv_b[at].astype(F32)).astype(BF16)
        scatter(scat_d, put_d[k], grad)

    head_ref[...] += dot_t(scat_d[...].astype(BF16), donor_w[...])

    @pl.loop(0, n - 1)
    def _(i):
        p = partner(i)
        rows_copy(send_a, recv_a, a_ssem, a_rsem, p, me).wait_send()
        rows_copy(send_b, recv_b, b_ssem, b_rsem, p, me).wait_send()


def on_device(
    features,
    bases,
    base_table,
    norm_gain,
    conv_weight,
    donor_proj,
    acceptor_proj,
    track_weight,
    donor_offset,
    acceptor_shard,
    acceptor_offset,
    junction_cotangent,
):
    n = lax.axis_size("seq")
    rows, channels = features.shape
    taps = conv_weight.shape[0]
    pair = donor_proj.shape[1]
    juncs = donor_offset.shape[0]
    cap = max(2 * juncs // n, 16)
    slots = n * cap
    tile = min(slots, 512)
    vmem = pl.BlockSpec(memory_space=pltpu.VMEM)
    hbm = pl.BlockSpec(memory_space=pl.ANY)
    dma = pltpu.SemaphoreType.DMA
    return pl.pallas_call(
        functools.partial(kernel, n, cap),
        out_shape=(
            jax.ShapeDtypeStruct((rows, channels), BF16),
            jax.ShapeDtypeStruct((rows, channels), F32),
        ),
        in_specs=[vmem, vmem, vmem, vmem, hbm, hbm, hbm, vmem, vmem, vmem, vmem, vmem],
        out_specs=(vmem, vmem),
        scratch_shapes=[
            pltpu.VMEM((rows + 2 * EDGE, channels), F32),
            pltpu.VMEM((rows, channels), F32),
            pltpu.VMEM((rows, taps * channels), BF16),
            pltpu.VMEM((taps * channels, channels), BF16),
            pltpu.VMEM((channels, pair), BF16),
            pltpu.VMEM((channels, pair), BF16),
            pltpu.VMEM((rows, pair), BF16),
            pltpu.VMEM((rows, pair), BF16),
            pltpu.VMEM((slots, pair), F32),
            pltpu.VMEM((slots, pair), BF16),
            pltpu.VMEM((slots, pair), BF16),
            pltpu.VMEM((slots, pair), BF16),
            pltpu.VMEM((slots, pair), BF16),
            pltpu.VMEM((n, 8, 128), I32),
            pltpu.VMEM((n, 8, 128), I32),
            pltpu.VMEM((slots, 128), I32),
            pltpu.VMEM((slots // tile, 8, tile), I32),
            pltpu.VMEM((slots, 128), I32),
            pltpu.VMEM((rows, pair), F32),
            pltpu.VMEM((rows, pair), F32),
            pltpu.VMEM((slots // tile, rows, tile), BF16),
            pltpu.VMEM((slots // tile, rows, tile), BF16),
            dma((taps + 2,)),
            dma((2,)),
            dma((2,)),
            dma((n,)),
            dma((n,)),
            dma((n,)),
            dma((n,)),
            dma((n,)),
            dma((n,)),
        ],
        compiler_params=pltpu.CompilerParams(
            collective_id=0, has_side_effects=True, vmem_limit_bytes=58 * 1024 * 1024
        ),
        name="block_and_pairs",
    )(
        features,
        bases.reshape(1, rows),
        base_table,
        norm_gain,
        conv_weight,
        donor_proj,
        acceptor_proj,
        track_weight,
        donor_offset.reshape(1, juncs),
        acceptor_shard.reshape(1, juncs),
        acceptor_offset.reshape(1, juncs),
        junction_cotangent,
    )


def solution(mesh):
    split = ("groups", "seq")
    in_specs = (
        P(split, None),
        P(split),
        P(),
        P(),
        P(),
        P(),
        P(),
        P(),
        P(split),
        P(split, None),
        P(split),
        P(split, None),
    )
    out_specs = (P(split, None), P(split, None))
    return jax.shard_map(
        on_device, mesh=mesh, in_specs=in_specs, out_specs=out_specs, check_vma=False
    )
```
